512 devices in a mesh: gx: 4 (over x), gy: 4 (over z_lo, core), gz: 32 (over z_hi, y).
Axes of the slice: x: 4, y: 8, z: 8 (z_hi: 4, z_lo: 2; z = z_hi * 2 + z_lo), core: 2. Of those that a mesh axis runs over, the one named last changes fastest.
Arguments:
- in_first: bfloat16 [262144, 1024], P(('gx', 'gy', 'gz')), may hold values from -98 to 98
- cot_first: bfloat16 [262144, 256], P(('gx', 'gy', 'gz')), may hold values from -0.05859375 to 0.05859375
- in_third: bfloat16 [262144, 256], P(('gx', 'gy', 'gz')), may hold values from -98 to 98
- cot_third: bfloat16 [262144, 1024], P(('gx', 'gy', 'gz')), may hold values from -0.05859375 to 0.05859375
- mean_old: float32 [524288], P(('gx', 'gy', 'gz')), may hold values from -6 to 6
- prec_old: float32 [524288], P(('gx', 'gy', 'gz')), may hold values from 0.5 to 4
- mom_old: float32 [524288], P(('gx', 'gy', 'gz')), may hold values from -4 to 4
- noise: bfloat16 [512, 524288], P(('gx', 'gy', 'gz')), may hold values from -6 to 6
Outputs:
- mean_new: float32 [524288], P(('gx', 'gy', 'gz'))
- prec_new: float32 [524288], P(('gx', 'gy', 'gz'))
- mom_new: float32 [524288], P(('gx', 'gy', 'gz'))
- samples: bfloat16 [512, 524288], P(('gx', 'gy', 'gz'))
The draws below stay inside these ranges and needn't reach their ends.
All inputs are finite; a program needn't handle non-finite values.
Results may differ from the reference program's by a relative error of at most 0.0016.
Values sent between devices are 32-bit elements; how exact they have to be, the bound alone decides.
No kernel may reach another device: no remote copies, remote signals or barrier semaphores. Data moves between devices by JAX's collectives and lax.ppermute only.
A program may use at most 64 MiB of HBM per device.

```python
import math
import jax
import jax.numpy as jnp
from jax import lax

CIN = 1024
MID = 256
TOKENS = 262144
PARAMS = 524288
DEVICES = 512


def section_fields(base_key, row_count, input_cols, output_cols):
    subkeys = jax.random.split(base_key, 7)
    heavy_share = 1.0 / 128.0
    heavy_scale = 5.0
    row_log = jax.random.uniform(subkeys[0], (row_count, 1), jnp.float32, -0.5, 0.5)
    row_tilt = jax.random.uniform(subkeys[1], (row_count, 1), jnp.float32, -1.0, 1.0)
    heavy_pick = jax.random.uniform(subkeys[2], (row_count, 1), jnp.float32, 0.0, 1.0)
    heavy_rows = jnp.where(heavy_pick < heavy_share, heavy_scale, 1.0).astype(jnp.float32)
    input_bend = jax.random.uniform(subkeys[3], (1, input_cols), jnp.float32, -0.5, 0.5)
    output_bend = jax.random.uniform(subkeys[4], (1, output_cols), jnp.float32, -0.5, 0.5)
    input_noise = jnp.clip(jax.random.normal(subkeys[5], (row_count, input_cols), jnp.float32), -6.0, 6.0)
    output_noise = jnp.clip(jax.random.normal(subkeys[6], (row_count, output_cols), jnp.float32), -6.0, 6.0)
    inputs_part = input_noise * heavy_rows * jnp.exp(row_log + row_tilt * input_bend)
    scaling = 0.3 / jnp.sqrt(jnp.float32(row_count))
    cotangents = output_noise * heavy_rows * jnp.exp(row_log + row_tilt * output_bend) * scaling
    return (inputs_part, cotangents)


def draw_in_first(key, part):
    fields = section_fields(jax.random.fold_in(key, 101), TOKENS, CIN, MID)
    return fields[0].astype(jnp.bfloat16)


def draw_cot_first(key, part):
    fields = section_fields(jax.random.fold_in(key, 101), TOKENS, CIN, MID)
    return fields[1].astype(jnp.bfloat16)


def draw_in_third(key, part):
    fields = section_fields(jax.random.fold_in(key, 202), TOKENS, MID, CIN)
    return fields[0].astype(jnp.bfloat16)


def draw_cot_third(key, part):
    fields = section_fields(jax.random.fold_in(key, 202), TOKENS, MID, CIN)
    return fields[1].astype(jnp.bfloat16)


def shard_levels(own_key, dims, cuts, least, largest):
    gain = 1.0
    for dim, shards_of in cuts:
        steps = jax.random.uniform(jax.random.fold_in(jax.random.fold_in(own_key, 6), dim), (shards_of,), jnp.float32, least / len(cuts), largest / len(cuts))
        gain = gain * jnp.repeat(jnp.exp(steps), dims[dim] // shards_of).reshape((-1,) + (1,) * (len(dims) - 1 - dim))
    return gain


def gaussian(own_key, extent, width, bound, cuts=(), held_as=jnp.bfloat16):
    values = jax.random.normal(own_key, extent, jnp.float32) * width
    if len(cuts) > 0:
        values = shard_levels(own_key, extent, cuts, -0.22, 0.18) * values
    return jnp.clip(values, min=-bound, max=bound).astype(held_as)


def setup_inputs(seed: int = 0) -> dict:
    seeds = jax.random.split(jax.random.key(seed), 9)
    return {
        "in_first": draw_in_first(jax.random.fold_in(seeds[8], 71), 0),
        "cot_first": draw_cot_first(jax.random.fold_in(seeds[8], 71), 0),
        "in_third": draw_in_third(jax.random.fold_in(seeds[8], 71), 0),
        "cot_third": draw_cot_third(jax.random.fold_in(seeds[8], 71), 0),
        "mean_old": gaussian(seeds[4], (PARAMS,), 1.0, 6.0, ((0, 512),), jnp.float32),
        "prec_old": jnp.clip(jnp.exp(math.log(4.0) - 2.0794415 * jax.random.uniform(seeds[5], (PARAMS,), jnp.float32) ** shard_levels(seeds[5], (PARAMS,), ((0, 512),), -0.2, 0.2)), 0.5, 4.0),
        "mom_old": gaussian(seeds[6], (PARAMS,), 0.5, 4.0, ((0, 512),), jnp.float32),
        "noise": gaussian(seeds[7], (DEVICES, PARAMS), 1.0, 6.0, ((0, 512),)),
    }


def squared(values):
    wide = values.astype(jnp.float32)
    return (wide * wide).astype(jnp.bfloat16)

def contract_rows(left, right):
    return lax.dot_general(left, right, (((0,), (0,)), ((), ())), preferred_element_type=jnp.float32)

def reference(in_first, cot_first, in_third, cot_third, mean_old, prec_old, mom_old, noise):
    grad_first = contract_rows(in_first, cot_first)
    grad_third = contract_rows(in_third, cot_third)
    curv_first = contract_rows(squared(in_first), squared(cot_first))
    curv_third = contract_rows(squared(in_third), squared(cot_third))
    grad = jnp.concatenate([grad_first.reshape(-1), grad_third.reshape(-1)])
    curv = jnp.concatenate([curv_first.reshape(-1), curv_third.reshape(-1)])
    prec_new = 0.5 * prec_old + 0.5 * curv
    mom_new = 0.9 * mom_old + grad + 0.1 * mean_old
    divisor = prec_new + 0.1 + 0.05
    mean_new = mean_old - 0.3 * mom_new / divisor
    spread = jnp.sqrt(0.3 / divisor)

    def one_sample(noise_row):
        return (mean_new + spread * noise_row.astype(jnp.float32)).astype(jnp.bfloat16)
    samples = lax.map(one_sample, noise)
    return (mean_new, prec_new, mom_new, samples)
```

```python
import functools

import numpy as np
import jax
import jax.numpy as jnp
from jax import lax
from jax.experimental import pallas as pl
from jax.experimental.pallas import tpu as pltpu
from jax.sharding import PartitionSpec as P

AXES = ("gx", "gy", "gz")
DEVICES = 512
SHARD = 1024
HALF = DEVICES // 2


def place(i):
    gx, gy, gz = i // 128, (i // 32) % 4, i % 32
    x, y, z = gx, gz % 8, (gz // 8) * 2 + gy // 2
    y1, z1 = (y + 1) % 8, (z + 1) % 8
    return {
        "c": gy % 2,
        "a": ((x + 1) >> 1) & 1, "b": x >> 1,
        "yh": y >> 1, "yl": y & 1, "zh": z >> 1, "zl": z & 1,
        "Yh": y1 >> 1, "Yl": y1 & 1, "Zh": z1 >> 1, "Zl": z1 & 1,
    }


PLACES = [place(i) for i in range(DEVICES)]
STAGES = (
    (("a", "yl", "zl"), ("b", "yh"), ("zh",)),
    (("b", "Yl", "Zl"), ("a", "Zh"), ("Yh",)),
)


def stage_groups(stage):
    groups = {}
    for i, p in enumerate(PLACES):
        digits = STAGES[p["c"]]
        rest = [d for s, ds in enumerate(digits) if s != stage for d in ds]
        key = (p["c"],) + tuple(p[d] for d in rest)
        groups.setdefault(key, []).append((tuple(p[d] for d in digits[stage]), i))
    return [[i for _, i in sorted(members)] for members in groups.values()]


GROUPS = [stage_groups(s) for s in range(3)]
ORDER = [
    [
        i
        for _, i in sorted(
            (tuple(p[d] for ds in STAGES[c] for d in ds), i)
            for i, p in enumerate(PLACES)
            if p["c"] == c
        )
    ]
    for c in range(2)
]
PARTNER = [(i, (i // 64) * 64 + (i + 32) % 64) for i in range(DEVICES)]


def selectors():
    first = np.zeros((2, 4, 128, 1024), np.float32)
    third = np.zeros((2, 128, 256), np.float32)
    for c in range(2):
        rows = [n for n in ORDER[c] if n < HALF]
        for r, n in enumerate(rows):
            for q in range(4):
                first[c, q, r, 4 * n + q] = 1
        rows = [n - HALF for n in ORDER[c] if n >= HALF]
        for r, n in enumerate(rows):
            third[c, r, n] = 1
    return first.reshape(2, 512, 1024), third


def mm(a, b, dims=((1,), (0,))):
    return lax.dot_general(a, b, (dims, ((), ())), preferred_element_type=jnp.float32)


def half_kernel(half_ref, in_first, cot_first, in_third, cot_third, pick_first, pick_third, out):
    half = half_ref[0]

    def base(b, g):
        return pl.multiple_of(jnp.where(half == 0, g * 32 + b * 16, b * 128 + g * 16), 16)

    def squares(v):
        return (v * v).astype(jnp.bfloat16)

    wide = cot_third[...].astype(jnp.float32)
    rows = mm(pick_third[0], in_third[...], ((1,), (1,)))
    grad = mm(rows.astype(jnp.bfloat16), cot_third[...])
    curv = mm(squares(rows), squares(wide))
    for g in range(8):
        out[pl.ds(base(1, g), 16), 0:1024] = grad[16 * g : 16 * g + 16]
        out[pl.ds(base(1, g), 16), 1024:2048] = curv[16 * g : 16 * g + 16]
    wide = cot_first[...].astype(jnp.float32)
    cot_sq = squares(wide)
    for q in range(4):
        rows = mm(pick_first[0, 128 * q : 128 * q + 128], in_first[...], ((1,), (1,)))
        grad = mm(rows.astype(jnp.bfloat16), cot_first[...])
        curv = mm(squares(rows), cot_sq)
        for g in range(8):
            out[pl.ds(base(0, g), 16), 256 * q : 256 * q + 256] = grad[16 * g : 16 * g + 16]
            out[pl.ds(base(0, g), 16), 1024 + 256 * q : 1280 + 256 * q] = curv[16 * g : 16 * g + 16]


def half_sums(half, in_first, cot_first, in_third, cot_third, pick_first, pick_third):
    def whole(*shape):
        return pl.BlockSpec(shape, lambda i, s: (0,) * len(shape))

    return pl.pallas_call(
        half_kernel,
        grid_spec=pltpu.PrefetchScalarGridSpec(
            num_scalar_prefetch=1,
            grid=(1,),
            in_specs=[
                whole(512, 1024), whole(512, 256), whole(512, 256), whole(512, 1024),
                pl.BlockSpec((1, 512, 1024), lambda i, s: (s[0], 0, 0)),
                pl.BlockSpec((1, 128, 256), lambda i, s: (s[0], 0, 0)),
            ],
            out_specs=whole(256, 2048),
        ),
        out_shape=jax.ShapeDtypeStruct((256, 2048), jnp.float32),
        compiler_params=pltpu.CompilerParams(vmem_limit_bytes=32 * 1024 * 1024),
        cost_estimate=pl.CostEstimate(flops=1_100_000_000, bytes_accessed=5_600_000, transcendentals=0),
        name="half_sums",
    )(half, in_first, cot_first, in_third, cot_third, pick_first, pick_third)


def order_kernel(core_ref, table, own, other, mean, spread):
    core = core_ref[0]

    def step(p, carry):
        mine, theirs = table[core, p], table[1 - core, p]
        mean[mine] = own[p, 0]
        spread[mine] = own[p, 1]
        mean[theirs] = other[p, 0]
        spread[theirs] = other[p, 1]
        return carry

    lax.fori_loop(0, HALF, step, 0, unroll=8)


def in_flat_order(core, own, other):
    table = jnp.asarray(np.array(ORDER, np.int32))
    shape = jax.ShapeDtypeStruct((DEVICES, 8, 128), jnp.float32)
    smem = pl.BlockSpec(memory_space=pltpu.SMEM)
    return pl.pallas_call(
        order_kernel,
        in_specs=[smem, smem, pl.BlockSpec(memory_space=pltpu.VMEM), pl.BlockSpec(memory_space=pltpu.VMEM)],
        out_specs=[pl.BlockSpec(memory_space=pltpu.VMEM)] * 2,
        out_shape=[shape, shape],
        compiler_params=pltpu.CompilerParams(vmem_limit_bytes=32 * 1024 * 1024),
        name="flat_order",
    )(core, table, own, other)


def exchanged(x, groups):
    return lax.all_to_all(x, AXES, 0, 0, axis_index_groups=groups, tiled=True)


def summed(x, groups):
    return exchanged(x, groups).sum(axis=0)


def from_all(x, groups):
    return exchanged(jnp.broadcast_to(x[None], (len(groups[0]), *x.shape)), groups)


def on_device(in_first, cot_first, in_third, cot_third, mean_old, prec_old, mom_old, noise):
    core = lax.axis_index("gy") % 2
    gz = lax.axis_index("gz")
    slot = jnp.where(core == 0, gz // 8, ((gz % 8 + 1) % 8) // 2)
    first, third = selectors()
    first, third = jnp.asarray(first, jnp.bfloat16), jnp.asarray(third, jnp.bfloat16)
    core_1 = core.astype(jnp.int32).reshape(1)
    send = half_sums(1 - core_1, in_first, cot_first, in_third, cot_third, first, third)
    arrived = lax.ppermute(send, AXES, PARTNER)
    keep = half_sums(core_1, in_first, cot_first, in_third, cot_third, first, third)
    sums = (keep + arrived).reshape(8, 32, 2048)
    sums = summed(sums, GROUPS[0]).reshape(8, 4, 2048)
    sums = summed(sums, GROUPS[1])
    state = jnp.concatenate([mean_old, prec_old, mom_old, mom_old]).reshape(2, 2048)
    parts = from_all(jnp.concatenate([sums, state, state], axis=0), GROUPS[2])
    total = parts[:, :4].sum(axis=0)
    grad, curv = total[:, :1024], total[:, 1024:]
    mean_4, prec_4, mom_4 = parts[:, 4, :1024], parts[:, 4, 1024:], parts[:, 5, :1024]
    prec_new = 0.5 * prec_4 + 0.5 * curv
    mom_new = 0.9 * mom_4 + grad + 0.1 * mean_4
    divisor = prec_new + 0.1 + 0.05
    mean_new = mean_4 - 0.3 * mom_new / divisor
    spread = jnp.sqrt(0.3 / divisor)
    posterior = jnp.stack([mean_new.reshape(4, 8, 128), spread.reshape(4, 8, 128)], axis=1)
    mine = [lax.dynamic_index_in_dim(v, slot, 0, keepdims=False) for v in (mean_new, prec_new, mom_new)]
    block = from_all(posterior, GROUPS[1]).reshape(32, 2, 8, 128)
    own = from_all(block, GROUPS[0]).reshape(256, 2, 8, 128)
    other = lax.ppermute(own, AXES, PARTNER)
    mean, spread = in_flat_order(core_1, own, other)
    sample_row = (mean.reshape(1, -1) + spread.reshape(1, -1) * noise.astype(jnp.float32)).astype(jnp.bfloat16)
    return (*mine, sample_row)


def solution(mesh):
    rows, flat = P(AXES, None), P(AXES)
    return jax.shard_map(
        on_device,
        mesh=mesh,
        in_specs=(rows, rows, rows, rows, flat, flat, flat, rows),
        out_specs=(flat, flat, flat, rows),
        check_vma=False,
    )
```

```python
import functools

import numpy as np
import jax
import jax.numpy as jnp
from jax import lax
from jax.experimental import pallas as pl
from jax.experimental.pallas import tpu as pltpu
from jax.sharding import PartitionSpec as P

AXES = ("gx", "gy", "gz")
DEVICES = 512
SHARD = 1024
HALF = DEVICES // 2


def place(i):
    gx, gy, gz = i // 128, (i // 32) % 4, i % 32
    x, y, z = gx, gz % 8, (gz // 8) * 2 + gy // 2
    y1, z1 = (y + 1) % 8, (z + 1) % 8
    return {
        "c": gy % 2,
        "a": ((x + 1) >> 1) & 1, "b": x >> 1,
        "yh": y >> 1, "yl": y & 1, "zh": z >> 1, "zl": z & 1,
        "Yh": y1 >> 1, "Yl": y1 & 1, "Zh": z1 >> 1, "Zl": z1 & 1,
    }


PLACES = [place(i) for i in range(DEVICES)]
STAGES = (
    (("a", "yl", "zl"), ("b", "yh"), ("zh",)),
    (("b", "Yl", "Zl"), ("a", "Zh"), ("Yh",)),
)


def stage_groups(stage):
    groups = {}
    for i, p in enumerate(PLACES):
        digits = STAGES[p["c"]]
        rest = [d for s, ds in enumerate(digits) if s != stage for d in ds]
        key = (p["c"],) + tuple(p[d] for d in rest)
        groups.setdefault(key, []).append((tuple(p[d] for d in digits[stage]), i))
    return [[i for _, i in sorted(members)] for members in groups.values()]


GROUPS = [stage_groups(s) for s in range(3)]
ORDER = [
    [
        i
        for _, i in sorted(
            (tuple(p[d] for ds in STAGES[c] for d in ds), i)
            for i, p in enumerate(PLACES)
            if p["c"] == c
        )
    ]
    for c in range(2)
]
PARTNER = [(i, (i // 64) * 64 + (i + 32) % 64) for i in range(DEVICES)]


def selectors():
    first = np.zeros((2, 4, 128, 1024), np.float32)
    third = np.zeros((2, 128, 256), np.float32)
    for c in range(2):
        rows = [n for n in ORDER[c] if n < HALF]
        for r, n in enumerate(rows):
            for q in range(4):
                first[c, q, r, 4 * n + q] = 1
        rows = [n - HALF for n in ORDER[c] if n >= HALF]
        for r, n in enumerate(rows):
            third[c, r, n] = 1
    return first.reshape(2, 512, 1024), third


def mm(a, b, dims=((1,), (0,))):
    return lax.dot_general(a, b, (dims, ((), ())), preferred_element_type=jnp.float32)


def half_body(half, in_first, cot_first, in_third, cot_third, pick_first, pick_third, out, ready):
    def base(b, g):
        return pl.multiple_of(jnp.where(half == 0, g * 32 + b * 16, b * 128 + g * 16), 16)

    def squares(v):
        return (v * v).astype(jnp.bfloat16)

    def spread_out(b, lane, width, grad, curv):
        for g in range(8):
            out[pl.ds(base(b, g), 16), lane : lane + width] = grad[16 * g : 16 * g + 16]
            out[pl.ds(base(b, g), 16), 1024 + lane : 1024 + lane + width] = curv[16 * g : 16 * g + 16]

    ready(0)
    rows = mm(pick_third[...], in_third[...], ((1,), (1,)))
    ready(1)
    wide = cot_third[...].astype(jnp.float32)
    grad = mm(rows.astype(jnp.bfloat16), cot_third[...])
    curv = mm(squares(rows), squares(wide))
    spread_out(1, 0, 1024, grad, curv)
    ready(2)
    wide = cot_first[...].astype(jnp.float32)
    cot_sq = squares(wide)
    for q in range(4):
        rows = mm(pick_first[128 * q : 128 * q + 128], in_first[...], ((1,), (1,)))
        grad = mm(rows.astype(jnp.bfloat16), cot_first[...])
        curv = mm(squares(rows), cot_sq)
        spread_out(0, 256 * q, 256, grad, curv)


def fetching_kernel(half_ref, in_first, cot_first, in_third, cot_third, pick_first, pick_third,
                    out, a, b, c, d, e, f, sems):
    half = half_ref[0]
    moves = [
        ((in_third, c), (pick_third.at[half], f)),
        ((cot_third, d),),
        ((cot_first, b), (in_first, a), (pick_first.at[half], e)),
    ]
    copies, at = [], 0
    for group in moves:
        copies.append([])
        for src, dst in group:
            copies[-1].append(pltpu.make_async_copy(src, dst, sems.at[at]))
            at += 1
    for group in copies:
        for copy in group:
            copy.start()

    def ready(stage):
        for copy in copies[stage]:
            copy.wait()

    half_body(half, a, b, c, d, e, f, out, ready)


def held_kernel(half_ref, in_first, cot_first, in_third, cot_third, pick_first, pick_third, out):
    half_body(half_ref[0], in_first, cot_first, in_third, cot_third, pick_first.at[0], pick_third.at[0],
              out, lambda stage: None)


SUMS = jax.ShapeDtypeStruct((256, 2048), jnp.float32)
COST = pl.CostEstimate(flops=1_100_000_000, bytes_accessed=5_600_000, transcendentals=0)
PARAMS = pltpu.CompilerParams(vmem_limit_bytes=32 * 1024 * 1024)
SMEM = pl.BlockSpec(memory_space=pltpu.SMEM)
VMEM = pl.BlockSpec(memory_space=pltpu.VMEM)
HBM = pl.BlockSpec(memory_space=pltpu.HBM)


def sums_to_send(half, *arrays):
    def buffer(*shape):
        return pltpu.VMEM(shape, jnp.bfloat16)

    return pl.pallas_call(
        fetching_kernel,
        in_specs=[SMEM] + [HBM] * 6,
        out_specs=VMEM,
        out_shape=SUMS,
        scratch_shapes=[
            buffer(512, 1024), buffer(512, 256), buffer(512, 256), buffer(512, 1024),
            buffer(512, 1024), buffer(128, 256), pltpu.SemaphoreType.DMA((6,)),
        ],
        compiler_params=pltpu.CompilerParams(vmem_limit_bytes=56 * 1024 * 1024),
        cost_estimate=COST,
        name="sums_to_send",
    )(half, *arrays)


def sums_to_keep(half, *arrays):
    def whole(*shape):
        return pl.BlockSpec(shape, lambda i, s: (0,) * len(shape))

    return pl.pallas_call(
        held_kernel,
        grid_spec=pltpu.PrefetchScalarGridSpec(
            num_scalar_prefetch=1,
            grid=(1,),
            in_specs=[
                whole(512, 1024), whole(512, 256), whole(512, 256), whole(512, 1024),
                pl.BlockSpec((1, 512, 1024), lambda i, s: (s[0], 0, 0)),
                pl.BlockSpec((1, 128, 256), lambda i, s: (s[0], 0, 0)),
            ],
            out_specs=whole(256, 2048),
        ),
        out_shape=SUMS,
        compiler_params=PARAMS,
        cost_estimate=COST,
        name="sums_to_keep",
    )(half, *arrays)


def sample_kernel(half_ref, table, noise, posterior, *refs):
    out, rows, sems = refs[-3:]
    half = half_ref[0]
    copies = []
    for run in range(8):
        first = (run >> 1) * 128 + (run & 1) * 64 + half * 32

        def step(j, carry, run=run, first=first):
            at = pl.ds(pl.multiple_of((first + j) * SHARD, SHARD), SHARD)
            p = table[half, run * 32 + j]
            normal = noise[0:1, at].astype(jnp.float32).reshape(8, 128)
            row = posterior[p, 0] + posterior[p, 1] * normal
            rows[0:1, at] = row.reshape(1, SHARD).astype(jnp.bfloat16)
            return carry

        lax.fori_loop(0, 32, step, 0, unroll=8)
        part = pl.ds(pl.multiple_of(first * SHARD, 32 * SHARD), 32 * SHARD)
        copies.append(pltpu.make_async_copy(rows.at[:, part], out.at[:, part], sems.at[run]))
        copies[-1].start()
    for copy in copies:
        copy.wait()


def sampled(half, noise, posterior, *begun):
    table = np.array([np.argsort(order) for order in ORDER], np.int32)
    return pl.pallas_call(
        sample_kernel,
        in_specs=[SMEM, SMEM, VMEM, VMEM] + [HBM] * len(begun),
        out_specs=HBM,
        out_shape=jax.ShapeDtypeStruct(noise.shape, jnp.bfloat16),
        scratch_shapes=[pltpu.VMEM(noise.shape, jnp.bfloat16), pltpu.SemaphoreType.DMA((8,))],
        input_output_aliases={4: 0} if begun else {},
        compiler_params=PARAMS,
        cost_estimate=pl.CostEstimate(flops=524288, bytes_accessed=4_200_000, transcendentals=0),
        name="sampled",
    )(half, jnp.asarray(table), noise, posterior, *begun)


def exchanged(x, groups):
    return lax.all_to_all(x, AXES, 0, 0, axis_index_groups=groups, tiled=True)


def summed(x, groups):
    return exchanged(x, groups).sum(axis=0)


def from_all(x, groups):
    return exchanged(jnp.broadcast_to(x[None], (len(groups[0]), *x.shape)), groups)


def on_device(in_first, cot_first, in_third, cot_third, mean_old, prec_old, mom_old, noise):
    core = lax.axis_index("gy") & 1
    gz = lax.axis_index("gz")
    slot = jnp.where(core == 0, gz >> 3, (((gz & 7) + 1) & 7) >> 1)
    first, third = selectors()
    arrays = (in_first, cot_first, in_third, cot_third, jnp.asarray(first, jnp.bfloat16), jnp.asarray(third, jnp.bfloat16))
    here = core.astype(jnp.int32).reshape(1)
    there = 1 - here
    send = sums_to_send(there, *arrays)
    arrived = lax.ppermute(send, AXES, PARTNER)
    keep = sums_to_keep(here, *arrays)
    state = jnp.concatenate([mean_old, prec_old, mom_old])
    state = jnp.where(jnp.arange(4)[:, None] == slot, state[None], 0.0)
    sums, state = lax.optimization_barrier((keep + arrived, state))
    sums = summed(sums.reshape(8, 32, 2048), GROUPS[0]).reshape(8, 4, 2048)
    sums = summed(sums, GROUPS[1])
    total = from_all(jnp.concatenate([sums, state], axis=1), GROUPS[2]).sum(axis=0)
    grad, curv, mean_4, prec_4, mom_4 = (total[:, 1024 * i : 1024 * (i + 1)] for i in range(5))
    prec_new = 0.5 * prec_4 + 0.5 * curv
    mom_new = 0.9 * mom_4 + grad + 0.1 * mean_4
    divisor = prec_new + 0.1 + 0.05
    mean_new = mean_4 - 0.3 * mom_new / divisor
    spread = jnp.sqrt(0.3 / divisor)
    posterior = jnp.stack([mean_new.reshape(4, 8, 128), spread.reshape(4, 8, 128)], axis=1)
    block = from_all(posterior, GROUPS[1]).reshape(32, 2, 8, 128)
    own = from_all(block, GROUPS[0]).reshape(256, 2, 8, 128)
    mine = [lax.dynamic_index_in_dim(v, slot, 0, keepdims=False) for v in (mean_new, prec_new, mom_new)]
    other = lax.ppermute(own, AXES, PARTNER)
    return (*mine, sampled(there, noise, other, sampled(here, noise, own)))


def solution(mesh):
    rows, flat = P(AXES, None), P(AXES)
    return jax.shard_map(
        on_device,
        mesh=mesh,
        in_specs=(rows, rows, rows, rows, flat, flat, flat, rows),
        out_specs=(flat, flat, flat, rows),
        check_vma=False,
    )
```

```python
import functools

import numpy as np
import jax
import jax.numpy as jnp
from jax import lax
from jax.experimental import pallas as pl
from jax.experimental.pallas import tpu as pltpu
from jax.sharding import PartitionSpec as P

AXES = ("gx", "gy", "gz")
DEVICES = 512
SHARD = 1024
HALF = DEVICES // 2


def place(i):
    gx, gy, gz = i // 128, (i // 32) % 4, i % 32
    x, y, z = gx, gz % 8, (gz // 8) * 2 + gy // 2
    y1, z1 = (y + 1) % 8, (z + 1) % 8
    return {
        "c": gy % 2,
        "a": ((x + 1) >> 1) & 1, "b": x >> 1,
        "yh": y >> 1, "yl": y & 1, "zh": z >> 1, "zl": z & 1,
        "Yh": y1 >> 1, "Yl": y1 & 1, "Zh": z1 >> 1, "Zl": z1 & 1,
    }


PLACES = [place(i) for i in range(DEVICES)]
STAGES = (
    (("a", "yl", "zl"), ("b", "yh"), ("zh",)),
    (("b", "Yl", "Zl"), ("a", "Zh"), ("Yh",)),
)


def stage_groups(stage):
    groups = {}
    for i, p in enumerate(PLACES):
        digits = STAGES[p["c"]]
        rest = [d for s, ds in enumerate(digits) if s != stage for d in ds]
        key = (p["c"],) + tuple(p[d] for d in rest)
        groups.setdefault(key, []).append((tuple(p[d] for d in digits[stage]), i))
    return [[i for _, i in sorted(members)] for members in groups.values()]


GROUPS = [stage_groups(s) for s in range(3)]
ORDER = [
    [
        i
        for _, i in sorted(
            (tuple(p[d] for ds in STAGES[c] for d in ds), i)
            for i, p in enumerate(PLACES)
            if p["c"] == c
        )
    ]
    for c in range(2)
]
PARTNER = [(i, (i // 64) * 64 + (i + 32) % 64) for i in range(DEVICES)]


def selectors():
    first = np.zeros((2, 4, 128, 1024), np.float32)
    third = np.zeros((2, 128, 256), np.float32)
    for c in range(2):
        rows = [n for n in ORDER[c] if n < HALF]
        for r, n in enumerate(rows):
            for q in range(4):
                first[c, q, r, 4 * n + q] = 1
        rows = [n - HALF for n in ORDER[c] if n >= HALF]
        for r, n in enumerate(rows):
            third[c, r, n] = 1
    return first.reshape(2, 512, 1024), third


def mm(a, b, dims=((1,), (0,))):
    return lax.dot_general(a, b, (dims, ((), ())), preferred_element_type=jnp.float32)


def half_body(half, in_first, cot_first, in_third, cot_third, pick_first, pick_third, out, ready):
    def base(b, g):
        return pl.multiple_of(jnp.where(half == 0, g * 32 + b * 16, b * 128 + g * 16), 16)

    def squares(v):
        return (v * v).astype(jnp.bfloat16)

    def spread_out(b, lane, width, grad, curv):
        for g in range(8):
            out[pl.ds(base(b, g), 16), lane : lane + width] = grad[16 * g : 16 * g + 16]
            out[pl.ds(base(b, g), 16), 1024 + lane : 1024 + lane + width] = curv[16 * g : 16 * g + 16]

    ready(0)
    rows = mm(pick_third[...], in_third[...], ((1,), (1,)))
    ready(1)
    wide = cot_third[...].astype(jnp.float32)
    grad = mm(rows.astype(jnp.bfloat16), cot_third[...])
    curv = mm(squares(rows), squares(wide))
    spread_out(1, 0, 1024, grad, curv)
    ready(2)
    wide = cot_first[...].astype(jnp.float32)
    cot_sq = squares(wide)
    for q in range(4):
        rows = mm(pick_first[128 * q : 128 * q + 128], in_first[...], ((1,), (1,)))
        grad = mm(rows.astype(jnp.bfloat16), cot_first[...])
        curv = mm(squares(rows), cot_sq)
        spread_out(0, 256 * q, 256, grad, curv)


def fetching_kernel(half_ref, in_first, cot_first, in_third, cot_third, pick_first, pick_third,
                    out, a, b, c, d, e, f, sems):
    half = half_ref[0]
    moves = [
        ((in_third, c), (pick_third.at[half], f)),
        ((cot_third, d),),
        ((cot_first, b), (in_first, a), (pick_first.at[half], e)),
    ]
    copies, at = [], 0
    for group in moves:
        copies.append([])
        for src, dst in group:
            copies[-1].append(pltpu.make_async_copy(src, dst, sems.at[at]))
            at += 1
    for group in copies:
        for copy in group:
            copy.start()

    def ready(stage):
        for copy in copies[stage]:
            copy.wait()

    half_body(half, a, b, c, d, e, f, out, ready)


def held_kernel(half_ref, in_first, cot_first, in_third, cot_third, pick_first, pick_third, out):
    half_body(half_ref[0], in_first, cot_first, in_third, cot_third, pick_first.at[0], pick_third.at[0],
              out, lambda stage: None)


SUMS = jax.ShapeDtypeStruct((256, 2048), jnp.float32)
COST = pl.CostEstimate(flops=1_100_000_000, bytes_accessed=5_600_000, transcendentals=0)
PARAMS = pltpu.CompilerParams(vmem_limit_bytes=16 * 1024 * 1024)
SAMPLE_PARAMS = pltpu.CompilerParams(vmem_limit_bytes=16 * 1024 * 1024)
SMEM = pl.BlockSpec(memory_space=pltpu.SMEM)
VMEM = pl.BlockSpec(memory_space=pltpu.VMEM)
HBM = pl.BlockSpec(memory_space=pltpu.HBM)


def sums_to_send(half, *arrays):
    def buffer(*shape):
        return pltpu.VMEM(shape, jnp.bfloat16)

    return pl.pallas_call(
        fetching_kernel,
        in_specs=[SMEM] + [HBM] * 6,
        out_specs=VMEM,
        out_shape=SUMS,
        scratch_shapes=[
            buffer(512, 1024), buffer(512, 256), buffer(512, 256), buffer(512, 1024),
            buffer(512, 1024), buffer(128, 256), pltpu.SemaphoreType.DMA((6,)),
        ],
        compiler_params=pltpu.CompilerParams(vmem_limit_bytes=56 * 1024 * 1024),
        cost_estimate=COST,
        name="sums_to_send",
    )(half, *arrays)


def sums_to_keep(half, *arrays):
    def whole(*shape):
        return pl.BlockSpec(shape, lambda i, s: (0,) * len(shape))

    return pl.pallas_call(
        held_kernel,
        grid_spec=pltpu.PrefetchScalarGridSpec(
            num_scalar_prefetch=1,
            grid=(1,),
            in_specs=[
                whole(512, 1024), whole(512, 256), whole(512, 256), whole(512, 1024),
                pl.BlockSpec((1, 512, 1024), lambda i, s: (s[0], 0, 0)),
                pl.BlockSpec((1, 128, 256), lambda i, s: (s[0], 0, 0)),
            ],
            out_specs=whole(256, 2048),
        ),
        out_shape=SUMS,
        compiler_params=PARAMS,
        cost_estimate=COST,
        name="sums_to_keep",
    )(half, *arrays)


def sample_kernel(half_ref, table, noise, posterior, *refs):
    out, rows, sems = refs[-3:]
    half = half_ref[0]
    copies = []
    for run in range(8):
        first = (run >> 1) * 128 + (run & 1) * 64 + half * 32

        def step(j, carry, run=run, first=first):
            at = pl.ds(pl.multiple_of((first + j) * SHARD, SHARD), SHARD)
            p = table[half, run * 32 + j]
            normal = noise[0:1, at].astype(jnp.float32).reshape(8, 128)
            row = posterior[p, 0] + posterior[p, 1] * normal
            rows[0:1, at] = row.reshape(1, SHARD).astype(jnp.bfloat16)
            return carry

        lax.fori_loop(0, 32, step, 0, unroll=32)
        part = pl.ds(pl.multiple_of(first * SHARD, 32 * SHARD), 32 * SHARD)
        copies.append(pltpu.make_async_copy(rows.at[:, part], out.at[:, part], sems.at[run]))
        copies[-1].start()
    for copy in copies:
        copy.wait()


def sampled(half, noise, posterior, *begun):
    table = np.array([np.argsort(order) for order in ORDER], np.int32)
    return pl.pallas_call(
        sample_kernel,
        in_specs=[SMEM, SMEM, VMEM, VMEM] + [HBM] * len(begun),
        out_specs=HBM,
        out_shape=jax.ShapeDtypeStruct(noise.shape, jnp.bfloat16),
        scratch_shapes=[pltpu.VMEM(noise.shape, jnp.bfloat16), pltpu.SemaphoreType.DMA((8,))],
        input_output_aliases={4: 0} if begun else {},
        compiler_params=SAMPLE_PARAMS,
        cost_estimate=pl.CostEstimate(flops=524288, bytes_accessed=4_200_000, transcendentals=0),
        name="sampled",
    )(half, jnp.asarray(table), noise, posterior, *begun)


def exchanged(x, groups):
    return lax.all_to_all(x, AXES, 0, 0, axis_index_groups=groups, tiled=True)


def summed(x, groups):
    return exchanged(x, groups).sum(axis=0)


def from_all(x, groups):
    return exchanged(jnp.broadcast_to(x[None], (len(groups[0]), *x.shape)), groups)


def on_device(in_first, cot_first, in_third, cot_third, mean_old, prec_old, mom_old, noise):
    core = lax.axis_index("gy") & 1
    gz = lax.axis_index("gz")
    slot = jnp.where(core == 0, gz >> 3, (((gz & 7) + 1) & 7) >> 1)
    first, third = selectors()
    arrays = (in_first, cot_first, in_third, cot_third, jnp.asarray(first, jnp.bfloat16), jnp.asarray(third, jnp.bfloat16))
    here = core.astype(jnp.int32).reshape(1)
    there = 1 - here
    send = sums_to_send(there, *arrays)
    arrived = lax.ppermute(send, AXES, PARTNER)
    keep = sums_to_keep(here, *arrays)
    own_row = jnp.broadcast_to((jnp.arange(4)[:, None] == slot).astype(jnp.float32), (4, SHARD))

    def in_own_row(v):
        return jnp.where(own_row > 0.5, v[None], 0.0)

    state = jnp.concatenate([in_own_row(0.9 * mom_old + 0.1 * mean_old), in_own_row(prec_old)], axis=1)
    sums, state, mean_row, own_row = lax.optimization_barrier((keep + arrived, state, in_own_row(mean_old), own_row))
    sums = summed(sums.reshape(8, 32, 2048), GROUPS[0]).reshape(8, 4, 2048)
    sums = summed(sums, GROUPS[1])
    total = from_all(jnp.concatenate([sums + state, mean_row], axis=1), GROUPS[2]).sum(axis=0)
    mom_new, mean_4 = total[:, :1024], total[:, 2048:]
    prec_new = 0.5 * total[:, 1024:2048]
    divisor = prec_new + 0.1 + 0.05
    mean_new = mean_4 - 0.3 * mom_new / divisor
    spread = jnp.sqrt(0.3 / divisor)
    posterior = jnp.stack([mean_new.reshape(4, 8, 128), spread.reshape(4, 8, 128)], axis=1)
    block = from_all(posterior, GROUPS[1]).reshape(32, 2, 8, 128)
    own = from_all(block, GROUPS[0]).reshape(256, 2, 8, 128)
    mine = [jnp.where(own_row > 0.5, v, 0.0).sum(axis=0) for v in (mean_new, prec_new, mom_new)]
    other = lax.ppermute(own, AXES, PARTNER)
    return (*mine, sampled(there, noise, other, sampled(here, noise, own)))


def solution(mesh):
    rows, flat = P(AXES, None), P(AXES)
    return jax.shard_map(
        on_device,
        mesh=mesh,
        in_specs=(rows, rows, rows, rows, flat, flat, flat, rows),
        out_specs=(flat, flat, flat, rows),
        check_vma=False,
    )
```

```python
import functools

import numpy as np
import jax
import jax.numpy as jnp
from jax import lax
from jax.experimental import pallas as pl
from jax.experimental.pallas import tpu as pltpu
from jax.sharding import PartitionSpec as P

AXES = ("gx", "gy", "gz")
DEVICES = 512
SHARD = 1024
HALF = DEVICES // 2


def place(i):
    gx, gy, gz = i // 128, (i // 32) % 4, i % 32
    x, y, z = gx, gz % 8, (gz // 8) * 2 + gy // 2
    y1, z1 = (y + 1) % 8, (z + 1) % 8
    return {
        "c": gy % 2,
        "a": ((x + 1) >> 1) & 1, "b": x >> 1,
        "yh": y >> 1, "yl": y & 1, "zh": z >> 1, "zl": z & 1,
        "Yh": y1 >> 1, "Yl": y1 & 1, "Zh": z1 >> 1, "Zl": z1 & 1,
    }


PLACES = [place(i) for i in range(DEVICES)]
STAGES = (
    (("a", "yl", "zl"), ("b", "yh"), ("zh",)),
    (("b", "Yl", "Zl"), ("a", "Zh"), ("Yh",)),
)


def stage_groups(stage):
    groups = {}
    for i, p in enumerate(PLACES):
        digits = STAGES[p["c"]]
        rest = [d for s, ds in enumerate(digits) if s != stage for d in ds]
        key = (p["c"],) + tuple(p[d] for d in rest)
        groups.setdefault(key, []).append((tuple(p[d] for d in digits[stage]), i))
    return [[i for _, i in sorted(members)] for members in groups.values()]


GROUPS = [stage_groups(s) for s in range(3)]
ORDER = [
    [
        i
        for _, i in sorted(
            (tuple(p[d] for ds in STAGES[c] for d in ds), i)
            for i, p in enumerate(PLACES)
            if p["c"] == c
        )
    ]
    for c in range(2)
]
PARTNER = [(i, (i // 64) * 64 + (i + 32) % 64) for i in range(DEVICES)]


def selectors():
    first = np.zeros((2, 4, 128, 1024), np.float32)
    third = np.zeros((2, 128, 256), np.float32)
    for c in range(2):
        rows = [n for n in ORDER[c] if n < HALF]
        for r, n in enumerate(rows):
            for q in range(4):
                first[c, q, r, 4 * n + q] = 1
        rows = [n - HALF for n in ORDER[c] if n >= HALF]
        for r, n in enumerate(rows):
            third[c, r, n] = 1
    return first.reshape(2, 512, 1024), third


def mm(a, b, dims=((1,), (0,))):
    return lax.dot_general(a, b, (dims, ((), ())), preferred_element_type=jnp.float32)


def half_body(half, in_first, cot_first, in_third, cot_third, pick_first, pick_third, out, ready):
    def base(b, g):
        return pl.multiple_of(jnp.where(half == 0, g * 32 + b * 16, b * 128 + g * 16), 16)

    def squares(v):
        return (v * v).astype(jnp.bfloat16)

    def spread_out(b, lane, width, grad, curv):
        for g in range(8):
            out[pl.ds(base(b, g), 16), lane : lane + width] = grad[16 * g : 16 * g + 16]
            out[pl.ds(base(b, g), 16), 1024 + lane : 1024 + lane + width] = curv[16 * g : 16 * g + 16]

    ready(0)
    rows = mm(pick_third[...], in_third[...], ((1,), (1,)))
    ready(1)
    wide = cot_third[...].astype(jnp.float32)
    grad = mm(rows.astype(jnp.bfloat16), cot_third[...])
    curv = mm(squares(rows), squares(wide))
    spread_out(1, 0, 1024, grad, curv)
    ready(2)
    wide = cot_first[...].astype(jnp.float32)
    cot_sq = squares(wide)
    for q in range(4):
        rows = mm(pick_first[128 * q : 128 * q + 128], in_first[...], ((1,), (1,)))
        grad = mm(rows.astype(jnp.bfloat16), cot_first[...])
        curv = mm(squares(rows), cot_sq)
        spread_out(0, 256 * q, 256, grad, curv)


def fetching_kernel(half_ref, in_first, cot_first, in_third, cot_third, pick_first, pick_third,
                    out, a, b, c, d, e, f, sems):
    half = half_ref[0]
    moves = [
        ((in_third, c), (pick_third.at[half], f)),
        ((cot_third, d),),
        ((cot_first, b), (in_first, a), (pick_first.at[half], e)),
    ]
    copies, at = [], 0
    for group in moves:
        copies.append([])
        for src, dst in group:
            copies[-1].append(pltpu.make_async_copy(src, dst, sems.at[at]))
            at += 1
    for group in copies:
        for copy in group:
            copy.start()

    def ready(stage):
        for copy in copies[stage]:
            copy.wait()

    half_body(half, a, b, c, d, e, f, out, ready)


def held_kernel(half_ref, in_first, cot_first, in_third, cot_third, pick_first, pick_third, out):
    half_body(half_ref[0], in_first, cot_first, in_third, cot_third, pick_first.at[0], pick_third.at[0],
              out, lambda stage: None)


SUMS = jax.ShapeDtypeStruct((256, 2048), jnp.float32)
COST = pl.CostEstimate(flops=1_100_000_000, bytes_accessed=5_600_000, transcendentals=0)
PARAMS = pltpu.CompilerParams(vmem_limit_bytes=48 * 1024 * 1024)
SAMPLE_PARAMS = pltpu.CompilerParams(vmem_limit_bytes=16 * 1024 * 1024)
SMEM = pl.BlockSpec(memory_space=pltpu.SMEM)
VMEM = pl.BlockSpec(memory_space=pltpu.VMEM)
HBM = pl.BlockSpec(memory_space=pltpu.HBM)


def sums_to_send(half, *arrays):
    def buffer(*shape):
        return pltpu.VMEM(shape, jnp.bfloat16)

    return pl.pallas_call(
        fetching_kernel,
        in_specs=[SMEM] + [HBM] * 6,
        out_specs=VMEM,
        out_shape=SUMS,
        scratch_shapes=[
            buffer(512, 1024), buffer(512, 256), buffer(512, 256), buffer(512, 1024),
            buffer(512, 1024), buffer(128, 256), pltpu.SemaphoreType.DMA((6,)),
        ],
        compiler_params=pltpu.CompilerParams(vmem_limit_bytes=56 * 1024 * 1024),
        cost_estimate=COST,
        name="sums_to_send",
    )(half, *arrays)


def sums_to_keep(half, *arrays):
    def whole(*shape):
        return pl.BlockSpec(shape, lambda i, s: (0,) * len(shape))

    return pl.pallas_call(
        held_kernel,
        grid_spec=pltpu.PrefetchScalarGridSpec(
            num_scalar_prefetch=1,
            grid=(1,),
            in_specs=[
                whole(512, 1024), whole(512, 256), whole(512, 256), whole(512, 1024),
                pl.BlockSpec((1, 512, 1024), lambda i, s: (s[0], 0, 0)),
                pl.BlockSpec((1, 128, 256), lambda i, s: (s[0], 0, 0)),
            ],
            out_specs=whole(256, 2048),
        ),
        out_shape=SUMS,
        compiler_params=PARAMS,
        cost_estimate=COST,
        name="sums_to_keep",
    )(half, *arrays)


def add_kernel(kept, arrived, out, held, sems):
    parts = [pl.ds(32 * i, 32) for i in range(8)]
    copies = [pltpu.make_async_copy(arrived.at[p], held.at[p], sems.at[i]) for i, p in enumerate(parts)]
    for copy in copies:
        copy.start()
    for copy, p in zip(copies, parts):
        copy.wait()
        out[p, :] = kept[p, :] + held[p, :]


def added(kept, arrived):
    return pl.pallas_call(
        add_kernel,
        in_specs=[VMEM, HBM],
        out_specs=VMEM,
        out_shape=SUMS,
        scratch_shapes=[pltpu.VMEM((256, 2048), jnp.float32), pltpu.SemaphoreType.DMA((8,))],
        compiler_params=SAMPLE_PARAMS,
        name="added",
    )(kept, arrived)


def sample_kernel(half_ref, table, noise, posterior, *refs):
    out, rows, sems = refs[-3:]
    half = half_ref[0]
    copies = []
    for run in range(8):
        first = (run >> 1) * 128 + (run & 1) * 64 + half * 32

        def step(j, carry, run=run, first=first):
            at = pl.ds(pl.multiple_of((first + j) * SHARD, SHARD), SHARD)
            p = table[half, run * 32 + j]
            normal = noise[0:1, at].astype(jnp.float32).reshape(8, 128)
            row = posterior[p, 0] + posterior[p, 1] * normal
            rows[0:1, at] = row.reshape(1, SHARD).astype(jnp.bfloat16)
            return carry

        lax.fori_loop(0, 32, step, 0, unroll=32)
        part = pl.ds(pl.multiple_of(first * SHARD, 32 * SHARD), 32 * SHARD)
        copies.append(pltpu.make_async_copy(rows.at[:, part], out.at[:, part], sems.at[run]))
        copies[-1].start()
    for copy in copies:
        copy.wait()


def sampled(half, noise, posterior, *begun):
    table = np.array([np.argsort(order) for order in ORDER], np.int32)
    return pl.pallas_call(
        sample_kernel,
        in_specs=[SMEM, SMEM, VMEM, VMEM] + [HBM] * len(begun),
        out_specs=HBM,
        out_shape=jax.ShapeDtypeStruct(noise.shape, jnp.bfloat16),
        scratch_shapes=[pltpu.VMEM(noise.shape, jnp.bfloat16), pltpu.SemaphoreType.DMA((8,))],
        input_output_aliases={4: 0} if begun else {},
        compiler_params=SAMPLE_PARAMS,
        cost_estimate=pl.CostEstimate(flops=524288, bytes_accessed=4_200_000, transcendentals=0),
        name="sampled",
    )(half, jnp.asarray(table), noise, posterior, *begun)


def exchanged(x, groups):
    return lax.all_to_all(x, AXES, 0, 0, axis_index_groups=groups, tiled=True)


def summed(x, groups):
    return exchanged(x, groups).sum(axis=0)


def from_all(x, groups):
    return exchanged(jnp.broadcast_to(x[None], (len(groups[0]), *x.shape)), groups)


def on_device(in_first, cot_first, in_third, cot_third, mean_old, prec_old, mom_old, noise):
    core = lax.axis_index("gy") & 1
    gz = lax.axis_index("gz")
    slot = jnp.where(core == 0, gz >> 3, (((gz & 7) + 1) & 7) >> 1)
    first, third = selectors()
    arrays = (in_first, cot_first, in_third, cot_third, jnp.asarray(first, jnp.bfloat16), jnp.asarray(third, jnp.bfloat16))
    here = core.astype(jnp.int32).reshape(1)
    there = 1 - here
    send = sums_to_send(there, *arrays)
    arrived = lax.ppermute(send, AXES, PARTNER)
    keep = sums_to_keep(here, *arrays)
    own_row = jnp.broadcast_to((jnp.arange(4)[:, None] == slot).astype(jnp.float32), (4, SHARD))

    def in_own_row(v):
        return jnp.where(own_row > 0.5, v[None], 0.0)

    state = jnp.concatenate([in_own_row(0.9 * mom_old + 0.1 * mean_old), in_own_row(prec_old)], axis=1)
    sums, state, mean_row, own_row = lax.optimization_barrier((added(keep, arrived), state, in_own_row(mean_old), own_row))
    sums = summed(sums.reshape(8, 32, 2048), GROUPS[0]).reshape(8, 4, 2048)
    sums = summed(sums, GROUPS[1])
    total = from_all(jnp.concatenate([sums + state, mean_row], axis=1), GROUPS[2]).sum(axis=0)
    mom_new, mean_4 = total[:, :1024], total[:, 2048:]
    prec_new = 0.5 * total[:, 1024:2048]
    divisor = prec_new + 0.1 + 0.05
    mean_new = mean_4 - 0.3 * mom_new / divisor
    spread = jnp.sqrt(0.3 / divisor)
    posterior = jnp.stack([mean_new.reshape(4, 8, 128), spread.reshape(4, 8, 128)], axis=1)
    block = from_all(posterior, GROUPS[1]).reshape(32, 2, 8, 128)
    own = from_all(block, GROUPS[0]).reshape(256, 2, 8, 128)
    mine = [jnp.where(own_row > 0.5, v, 0.0).sum(axis=0) for v in (mean_new, prec_new, mom_new)]
    other = lax.ppermute(own, AXES, PARTNER)
    return (*mine, sampled(there, noise, other, sampled(here, noise, own)))


def solution(mesh):
    rows, flat = P(AXES, None), P(AXES)
    return jax.shard_map(
        on_device,
        mesh=mesh,
        in_specs=(rows, rows, rows, rows, flat, flat, flat, rows),
        out_specs=(flat, flat, flat, rows),
        check_vma=False,
    )
```

```python
import functools

import numpy as np
import jax
import jax.numpy as jnp
from jax import lax
from jax.experimental import pallas as pl
from jax.experimental.pallas import tpu as pltpu
from jax.sharding import PartitionSpec as P

AXES = ("gx", "gy", "gz")
DEVICES = 512
SHARD = 1024
HALF = DEVICES // 2


def place(i):
    gx, gy, gz = i // 128, (i // 32) % 4, i % 32
    x, y, z = gx, gz % 8, (gz // 8) * 2 + gy // 2
    y1, z1 = (y + 1) % 8, (z + 1) % 8
    return {
        "c": gy % 2,
        "a": ((x + 1) >> 1) & 1, "b": x >> 1,
        "yh": y >> 1, "yl": y & 1, "zh": z >> 1, "zl": z & 1,
        "Yh": y1 >> 1, "Yl": y1 & 1, "Zh": z1 >> 1, "Zl": z1 & 1,
    }


PLACES = [place(i) for i in range(DEVICES)]
STAGES = (
    (("a", "yl", "zl"), ("b", "yh"), ("zh",)),
    (("b", "Yl", "Zl"), ("a", "Zh"), ("Yh",)),
)


def stage_groups(stage):
    groups = {}
    for i, p in enumerate(PLACES):
        digits = STAGES[p["c"]]
        rest = [d for s, ds in enumerate(digits) if s != stage for d in ds]
        key = (p["c"],) + tuple(p[d] for d in rest)
        groups.setdefault(key, []).append((tuple(p[d] for d in digits[stage]), i))
    return [[i for _, i in sorted(members)] for members in groups.values()]


GROUPS = [stage_groups(s) for s in range(3)]
ORDER = [
    [
        i
        for _, i in sorted(
            (tuple(p[d] for ds in STAGES[c] for d in ds), i)
            for i, p in enumerate(PLACES)
            if p["c"] == c
        )
    ]
    for c in range(2)
]
PARTNER = [(i, (i // 64) * 64 + (i + 32) % 64) for i in range(DEVICES)]


def selectors():
    first = np.zeros((2, 4, 128, 1024), np.float32)
    third = np.zeros((2, 128, 256), np.float32)
    for c in range(2):
        rows = [n for n in ORDER[c] if n < HALF]
        for r, n in enumerate(rows):
            for q in range(4):
                first[c, q, r, 4 * n + q] = 1
        rows = [n - HALF for n in ORDER[c] if n >= HALF]
        for r, n in enumerate(rows):
            third[c, r, n] = 1
    return first.reshape(2, 512, 1024), third


def mm(a, b, dims=((1,), (0,))):
    return lax.dot_general(a, b, (dims, ((), ())), preferred_element_type=jnp.float32)


def half_body(half, in_first, cot_first, in_third, cot_third, pick_first, pick_third, out, ready, written):
    def base(b, g):
        return pl.multiple_of(jnp.where(half == 0, g * 32 + b * 16, b * 128 + g * 16), 16)

    def squares(v):
        return (v * v).astype(jnp.bfloat16)

    def spread_out(b, lane, width, grad, curv):
        for g in range(8):
            out[pl.ds(base(b, g), 16), lane : lane + width] = grad[16 * g : 16 * g + 16]
            out[pl.ds(base(b, g), 16), 1024 + lane : 1024 + lane + width] = curv[16 * g : 16 * g + 16]

    ready(0)
    rows = mm(pick_third[...], in_third[...], ((1,), (1,)))
    ready(1)
    wide = cot_third[...].astype(jnp.float32)
    grad = mm(rows.astype(jnp.bfloat16), cot_third[...])
    curv = mm(squares(rows), squares(wide))
    spread_out(1, 0, 1024, grad, curv)
    written([base(1, g) for g in range(8)])
    ready(2)
    wide = cot_first[...].astype(jnp.float32)
    cot_sq = squares(wide)
    for q in range(4):
        rows = mm(pick_first[128 * q : 128 * q + 128], in_first[...], ((1,), (1,)))
        grad = mm(rows.astype(jnp.bfloat16), cot_first[...])
        curv = mm(squares(rows), cot_sq)
        spread_out(0, 256 * q, 256, grad, curv)
    written([base(0, g) for g in range(8)])


def fetching_kernel(half_ref, in_first, cot_first, in_third, cot_third, pick_first, pick_third,
                    out, a, b, c, d, e, f, sums, sems, out_sems):
    half = half_ref[0]
    moves = [
        ((in_third, c), (pick_third.at[half], f)),
        ((cot_third, d),),
        ((cot_first, b), (in_first, a), (pick_first.at[half], e)),
    ]
    copies, at = [], 0
    for group in moves:
        copies.append([])
        for src, dst in group:
            copies[-1].append(pltpu.make_async_copy(src, dst, sems.at[at]))
            at += 1
    for group in copies:
        for copy in group:
            copy.start()

    def ready(stage):
        for copy in copies[stage]:
            copy.wait()

    leaving = []

    def written(bases):
        for at in bases:
            block = pl.ds(at, 16)
            leaving.append(pltpu.make_async_copy(sums.at[block], out.at[block], out_sems.at[len(leaving)]))
            leaving[-1].start()

    half_body(half, a, b, c, d, e, f, sums, ready, written)
    for copy in leaving:
        copy.wait()


def held_kernel(half_ref, in_first, cot_first, in_third, cot_third, pick_first, pick_third, out):
    half_body(half_ref[0], in_first, cot_first, in_third, cot_third, pick_first.at[0], pick_third.at[0],
              out, lambda stage: None, lambda bases: None)


SUMS = jax.ShapeDtypeStruct((256, 2048), jnp.float32)
COST = pl.CostEstimate(flops=1_100_000_000, bytes_accessed=5_600_000, transcendentals=0)
PARAMS = pltpu.CompilerParams(vmem_limit_bytes=48 * 1024 * 1024)
SAMPLE_PARAMS = pltpu.CompilerParams(vmem_limit_bytes=16 * 1024 * 1024)
SMEM = pl.BlockSpec(memory_space=pltpu.SMEM)
VMEM = pl.BlockSpec(memory_space=pltpu.VMEM)
HBM = pl.BlockSpec(memory_space=pltpu.HBM)


def sums_to_send(half, *arrays):
    def buffer(*shape):
        return pltpu.VMEM(shape, jnp.bfloat16)

    return pl.pallas_call(
        fetching_kernel,
        in_specs=[SMEM] + [HBM] * 6,
        out_specs=HBM,
        out_shape=SUMS,
        scratch_shapes=[
            buffer(512, 1024), buffer(512, 256), buffer(512, 256), buffer(512, 1024),
            buffer(512, 1024), buffer(128, 256), pltpu.VMEM((256, 2048), jnp.float32),
            pltpu.SemaphoreType.DMA((6,)), pltpu.SemaphoreType.DMA((16,)),
        ],
        compiler_params=pltpu.CompilerParams(vmem_limit_bytes=56 * 1024 * 1024),
        cost_estimate=COST,
        name="sums_to_send",
    )(half, *arrays)


def sums_to_keep(half, *arrays):
    def whole(*shape):
        return pl.BlockSpec(shape, lambda i, s: (0,) * len(shape))

    return pl.pallas_call(
        held_kernel,
        grid_spec=pltpu.PrefetchScalarGridSpec(
            num_scalar_prefetch=1,
            grid=(1,),
            in_specs=[
                whole(512, 1024), whole(512, 256), whole(512, 256), whole(512, 1024),
                pl.BlockSpec((1, 512, 1024), lambda i, s: (s[0], 0, 0)),
                pl.BlockSpec((1, 128, 256), lambda i, s: (s[0], 0, 0)),
            ],
            out_specs=whole(256, 2048),
        ),
        out_shape=SUMS,
        compiler_params=PARAMS,
        cost_estimate=COST,
        name="sums_to_keep",
    )(half, *arrays)


def add_kernel(kept, arrived, out, held, sems):
    parts = [pl.ds(32 * i, 32) for i in range(8)]
    copies = [pltpu.make_async_copy(arrived.at[p], held.at[p], sems.at[i]) for i, p in enumerate(parts)]
    for copy in copies:
        copy.start()
    for copy, p in zip(copies, parts):
        copy.wait()
        out[p, :] = kept[p, :] + held[p, :]


def added(kept, arrived):
    return pl.pallas_call(
        add_kernel,
        in_specs=[VMEM, HBM],
        out_specs=VMEM,
        out_shape=SUMS,
        scratch_shapes=[pltpu.VMEM((256, 2048), jnp.float32), pltpu.SemaphoreType.DMA((8,))],
        compiler_params=SAMPLE_PARAMS,
        name="added",
    )(kept, arrived)


def sample_kernel(half_ref, table, noise, posterior, *refs):
    out, rows, sems = refs[-3:]
    half = half_ref[0]
    copies = []
    for run in range(8):
        first = (run >> 1) * 128 + (run & 1) * 64 + half * 32

        def step(j, carry, run=run, first=first):
            at = pl.ds(pl.multiple_of((first + 4 * j) * SHARD, 4 * SHARD), 4 * SHARD)
            normal = noise[0:1, at].astype(jnp.float32).reshape(8 * 4, 128)
            rows_of = []
            for k in range(4):
                p = table[half, run * 32 + 4 * j + k]
                rows_of.append(posterior[p, 0] + posterior[p, 1] * normal[8 * k : 8 * k + 8])
            row = jnp.concatenate(rows_of, axis=0)
            rows[0:1, at] = row.reshape(1, 4 * SHARD).astype(jnp.bfloat16)
            return carry

        lax.fori_loop(0, 32 // 4, step, 0, unroll=32 // 4)
        part = pl.ds(pl.multiple_of(first * SHARD, 32 * SHARD), 32 * SHARD)
        copies.append(pltpu.make_async_copy(rows.at[:, part], out.at[:, part], sems.at[run]))
        copies[-1].start()
    for copy in copies:
        copy.wait()


def sampled(half, noise, posterior, *begun):
    table = np.array([np.argsort(order) for order in ORDER], np.int32)
    return pl.pallas_call(
        sample_kernel,
        in_specs=[SMEM, SMEM, VMEM, VMEM] + [HBM] * len(begun),
        out_specs=HBM,
        out_shape=jax.ShapeDtypeStruct(noise.shape, jnp.bfloat16),
        scratch_shapes=[pltpu.VMEM(noise.shape, jnp.bfloat16), pltpu.SemaphoreType.DMA((8,))],
        input_output_aliases={4: 0} if begun else {},
        compiler_params=SAMPLE_PARAMS,
        cost_estimate=pl.CostEstimate(flops=524288, bytes_accessed=4_200_000, transcendentals=0),
        name="sampled",
    )(half, jnp.asarray(table), noise, posterior, *begun)


def exchanged(x, groups):
    return lax.all_to_all(x, AXES, 0, 0, axis_index_groups=groups, tiled=True)


def summed(x, groups):
    return exchanged(x, groups).sum(axis=0)


def from_all(x, groups):
    return exchanged(jnp.broadcast_to(x[None], (len(groups[0]), *x.shape)), groups)


def on_device(in_first, cot_first, in_third, cot_third, mean_old, prec_old, mom_old, noise):
    core = lax.axis_index("gy") & 1
    gz = lax.axis_index("gz")
    slot = jnp.where(core == 0, gz >> 3, (((gz & 7) + 1) & 7) >> 1)
    first, third = selectors()
    arrays = (in_first, cot_first, in_third, cot_third, jnp.asarray(first, jnp.bfloat16), jnp.asarray(third, jnp.bfloat16))
    here = core.astype(jnp.int32).reshape(1)
    there = 1 - here
    send = sums_to_send(there, *arrays)
    arrived = lax.ppermute(send, AXES, PARTNER)
    keep = sums_to_keep(here, *arrays)
    own_row = jnp.broadcast_to((jnp.arange(4)[:, None] == slot).astype(jnp.float32), (4, SHARD))

    def in_own_row(v):
        return jnp.where(own_row > 0.5, v[None], 0.0)

    state = jnp.concatenate([in_own_row(0.9 * mom_old + 0.1 * mean_old), in_own_row(prec_old)], axis=1)
    sums, state, mean_row, own_row = lax.optimization_barrier((added(keep, arrived), state, in_own_row(mean_old), own_row))
    sums = summed(sums.reshape(8, 32, 2048), GROUPS[0]).reshape(8, 4, 2048)
    sums = summed(sums, GROUPS[1])
    total = from_all(jnp.concatenate([sums + state, mean_row], axis=1), GROUPS[2]).sum(axis=0)
    mom_new, mean_4 = total[:, :1024], total[:, 2048:]
    prec_new = 0.5 * total[:, 1024:2048]
    divisor = prec_new + 0.1 + 0.05
    mean_new = mean_4 - 0.3 * mom_new / divisor
    spread = jnp.sqrt(0.3 / divisor)
    posterior = jnp.stack([mean_new.reshape(4, 8, 128), spread.reshape(4, 8, 128)], axis=1)
    block = from_all(posterior, GROUPS[1]).reshape(32, 2, 8, 128)
    own = from_all(block, GROUPS[0]).reshape(256, 2, 8, 128)
    mine = [jnp.where(own_row > 0.5, v, 0.0).sum(axis=0) for v in (mean_new, prec_new, mom_new)]
    other = lax.ppermute(own, AXES, PARTNER)
    return (*mine, sampled(there, noise, other, sampled(here, noise, own)))


def solution(mesh):
    rows, flat = P(AXES, None), P(AXES)
    return jax.shard_map(
        on_device,
        mesh=mesh,
        in_specs=(rows, rows, rows, rows, flat, flat, flat, rows),
        out_specs=(flat, flat, flat, rows),
        check_vma=False,
    )
```
